256 devices in a mesh: rows: 32 (over z_lo, x, core), sub: 8 (over y, z_hi).
Axes of the slice: x: 4, y: 4, z: 8 (z_hi: 2, z_lo: 4; z = z_hi * 4 + z_lo), core: 2. Of those that a mesh axis runs over, the one named last changes fastest.
Arguments:
- embeddings: bfloat16 [16384, 1024], P('rows', 'sub'), may hold values from -40 to 40
- rotation: bfloat16 [1024, 1024], P(None, 'sub'), may hold values from -0.1875 to 0.1875
- codebooks: float32 [64, 16, 256], P('sub'), may hold values from -6 to 6
Outputs:
- new_codebooks: float32 [64, 16, 256], P('sub')
- new_rotation: float32 [1024, 1024], P('rows', 'sub')
The draws below stay inside these ranges and needn't reach their ends.
All inputs are finite; a program needn't handle non-finite values.
Results may differ from the reference program's by a relative error of at most 0.006.
The reference program's roundings to bfloat16 on the way count: a program that leaves them out, or rounds other values in their place, can miss the bound.
Values may be sent and summed in bfloat16 or wider, within the bound.
No kernel may reach another device: no remote copies, remote signals or barrier semaphores. Data moves between devices by JAX's collectives and lax.ppermute only.
A program may use at most 64 MiB of HBM per device.

```python
import jax
import jax.numpy as jnp
from jax import lax

D = 1024
SUBS = 64
CODES = 256
SUB_DIM = 16
ROW_DEV = 512
ITERS = 2
POLAR_ITER_COUNT = 2
ROWS = 16384
N_ROWS = 32


def draw_embeddings(key, part):
    base_key = jax.random.fold_in(key, 11)
    values = jax.random.normal(jax.random.fold_in(base_key, 1), (ROWS, D), jnp.float32)
    scale_key = jax.random.fold_in(base_key, 2)
    scales = jnp.exp(jax.random.uniform(scale_key, (ROWS, 1), jnp.float32, -1.2, 1.2))
    values = values * scales
    return jnp.clip(values, -40.0, 40.0).astype(jnp.bfloat16)


def block_scale(key, dims, cuts, low, top_value):
    gain = 1.0
    for dim, parts in cuts:
        heights = jax.random.uniform(jax.random.fold_in(jax.random.fold_in(key, 6), dim), (parts,), jnp.float32, low / len(cuts), top_value / len(cuts))
        gain = gain * jnp.repeat(jnp.exp(heights), dims[dim] // parts).reshape((-1,) + (1,) * (len(dims) - 1 - dim))
    return gain


def bell_draw(key, shape, deviation, bound, cuts=(), dtype=jnp.bfloat16):
    drawn = deviation * jax.random.normal(key, shape, jnp.float32)
    if cuts:
        drawn = drawn * block_scale(key, shape, cuts, -0.22, 0.18)
    return jnp.clip(drawn, -bound, bound).astype(dtype)


def setup_inputs(seed: int = 0) -> dict:
    streams_of = jax.random.split(jax.random.key(seed), 4)
    return {
        "embeddings": draw_embeddings(jax.random.fold_in(streams_of[3], 71), 0),
        "rotation": bell_draw(streams_of[1], (D, D), D ** -0.5, 0.1875, ((1, 8),)),
        "codebooks": bell_draw(streams_of[2], (SUBS, SUB_DIM, CODES), 1.0, 6.0, ((0, 8),), jnp.float32),
    }


softness_level = 4.0
prior_weight = 8.0
quintic_one = 3.4445
quintic_three = -4.775
quintic_five = 2.0315

def soft_weights(row_block, centroid_tables):
    pieces = row_block.reshape(row_block.shape[0], SUBS, SUB_DIM).astype(jnp.float32)
    codes_low = lax.optimization_barrier(centroid_tables.astype(jnp.bfloat16)).astype(jnp.float32)
    cross_products = jnp.einsum('bmd,mdk->bmk', pieces, codes_low)
    centroid_logits = (2.0 * cross_products - lax.optimization_barrier(jnp.sum(centroid_tables * centroid_tables, axis=1))[None]) / softness_level
    return jax.nn.softmax(centroid_logits, axis=-1).astype(jnp.bfloat16)

def reference(embeddings, rotation, codebooks):
    rotated = jnp.dot(embeddings, rotation, preferred_element_type=jnp.float32).astype(jnp.bfloat16)
    row_blocks = rotated.reshape(N_ROWS, ROW_DEV, D)
    books_now = codebooks
    books_prev = codebooks
    for repeat in range(ITERS):

        def gather_stats(running, row_block):
            weights = soft_weights(row_block, books_now).astype(jnp.float32)
            pieces = row_block.reshape(ROW_DEV, SUBS, SUB_DIM).astype(jnp.float32)
            return ((running[0] + lax.optimization_barrier(jnp.sum(weights, axis=0)), running[1] + jnp.einsum('bmd,bmk->mdk', pieces, weights)), None)
        start_vals = (jnp.zeros((SUBS, CODES), jnp.float32), jnp.zeros((SUBS, SUB_DIM, CODES), jnp.float32))
        (counts, totals), _ = lax.scan(gather_stats, start_vals, row_blocks)
        books_prev = books_now
        books_now = (totals + prior_weight * books_now) / (counts[:, None, :] + prior_weight)
    codes_low = lax.optimization_barrier(books_now.astype(jnp.bfloat16)).astype(jnp.float32)
    x_blocks = embeddings.reshape(N_ROWS, ROW_DEV, D)

    def add_cross(running, paired):
        row_block, x_block = paired
        weights = soft_weights(row_block, books_prev).astype(jnp.float32)
        rebuilt = jnp.einsum('bmk,mdk->bmd', weights, codes_low).reshape(ROW_DEV, D).astype(jnp.bfloat16)
        return (running + jnp.dot(x_block.T, rebuilt, preferred_element_type=jnp.float32), None)
    cross_products, _ = lax.scan(add_cross, jnp.zeros((D, D), jnp.float32), (row_blocks, x_blocks))
    frob_norm = jnp.sqrt(jnp.sum(cross_products * cross_products) + 1e-06)
    polar_now = cross_products / frob_norm
    for polar_rotation_step in range(POLAR_ITER_COUNT):
        gram = jnp.dot(polar_now, polar_now.T, precision=lax.Precision.HIGHEST)
        image = jnp.dot(gram, polar_now, precision=lax.Precision.HIGHEST)
        second = jnp.dot(gram, image, precision=lax.Precision.HIGHEST)
        polar_now = quintic_one * polar_now + quintic_three * image + quintic_five * second
    return (books_now, polar_now)
```

```python
import jax
import jax.numpy as jnp
from jax import lax
from jax.experimental import pallas as pl
from jax.experimental.pallas import tpu as pltpu
from jax.sharding import PartitionSpec as P

SUB_DIM = 16
CODES = 256
SOFTNESS = 4.0
PRIOR = 8.0
Q1, Q3, Q5 = 3.4445, -4.775, 2.0315

ROW_DEVS = 32
SUB_DEVS = 8
CHIPS = [[8 * z + 2 * x + c for z in range(4) for x in range(4)] for c in range(2)]

f32 = jnp.float32
bf16 = jnp.bfloat16
VMEM_LIMIT = 48 * 1024 * 1024


def call(kernel, out_shape, n_scalars, n_arrays, scratch=()):
    return pl.pallas_call(
        kernel,
        out_shape=out_shape,
        in_specs=[pl.BlockSpec(memory_space=pltpu.SMEM)] * n_scalars
        + [pl.BlockSpec(memory_space=pltpu.VMEM)] * n_arrays,
        scratch_shapes=list(scratch),
        compiler_params=pltpu.CompilerParams(vmem_limit_bytes=VMEM_LIMIT),
    )


def shape(dims, dtype):
    return jax.ShapeDtypeStruct(dims, dtype)


def dot(a, b, dims=((1,), (0,)), precision=None):
    return lax.dot_general(a, b, (dims, ((), ())), precision=precision, preferred_element_type=f32)


def permute_rows(x, to):
    return lax.ppermute(x, "rows", [(i, to(i)) for i in range(ROW_DEVS)])


def other_core(x):
    return permute_rows(x, lambda i: i ^ 1)


def gather_by_exchange(x, axis, count, groups=None):
    copies = jnp.broadcast_to(x[None], (count,) + x.shape)
    return lax.all_to_all(copies, axis, 0, 0, tiled=True, axis_index_groups=groups)


def rotate_kernel(core_ref, e_ref, r_ref, keep_ref, send_ref):
    full = jnp.concatenate([e_ref[s] for s in range(SUB_DEVS)], axis=1)
    rot = dot(full, r_ref[...]).T.astype(bf16)
    half = rot.shape[0] // 2
    first = core_ref[0] == 0
    keep_ref[...] = jnp.where(first, rot[:half], rot[half:])
    send_ref[...] = jnp.where(first, rot[half:], rot[:half])


def assign(book, feats):
    sq = 0.25 * jnp.sum(book * book, axis=0, keepdims=True)
    sq_a = sq.astype(bf16).astype(f32)
    sq_b = (sq - sq_a).astype(bf16).astype(f32)
    sq_c = (sq - sq_a) - sq_b
    low = book.astype(bf16).astype(f32)
    pad = jnp.zeros((SUB_DIM - 3, book.shape[1]), f32)
    lhs = jnp.concatenate([0.5 * low, -sq_a, -sq_b, -sq_c, pad], axis=0).T.astype(bf16)
    rhs = jnp.concatenate([feats, jnp.ones_like(feats)], axis=0)
    logits = dot(lhs, rhs)
    e = jnp.exp(logits - jnp.max(logits, axis=0, keepdims=True))
    w = (e * (1.0 / jnp.sum(e, axis=0, keepdims=True))).astype(bf16)
    stats = dot(rhs, w, ((1,), (1,)))
    return w, stats


def write_stats(stats_ref, m, n_sub, stats):
    stats_ref[SUB_DIM * m : SUB_DIM * (m + 1)] = stats[:SUB_DIM]
    stats_ref[SUB_DIM * n_sub + m : SUB_DIM * n_sub + m + 1] = stats[SUB_DIM : SUB_DIM + 1]


def first_kernel(core_ref, keep_ref, recv_ref, book_ref, stats_ref):
    n_sub = keep_ref.shape[0] // SUB_DIM
    feats = jnp.concatenate([keep_ref[...], recv_ref[...]], axis=1)
    stats_ref[...] = jnp.zeros_like(stats_ref)
    for m in range(n_sub):
        _, stats = assign(book_ref[core_ref[0] * n_sub + m], feats[SUB_DIM * m : SUB_DIM * (m + 1)])
        write_stats(stats_ref, m, n_sub, stats)


def new_book(a, b, c, d, m, n_sub, book):
    rows = slice(SUB_DIM * m, SUB_DIM * (m + 1))
    row = slice(SUB_DIM * n_sub + m, SUB_DIM * n_sub + m + 1)
    totals = (a[rows] + b[rows]) + (c[rows] + d[rows])
    counts = (a[row] + b[row]) + (c[row] + d[row])
    return (totals + PRIOR * book) / (counts + PRIOR)


def second_kernel(core_ref, keep_ref, recv_ref, book_ref, a, b, c, d, book_out, w_ref, stats_ref):
    n_sub = keep_ref.shape[0] // SUB_DIM
    feats = jnp.concatenate([keep_ref[...], recv_ref[...]], axis=1)
    stats_ref[...] = jnp.zeros_like(stats_ref)
    for m in range(n_sub):
        book = new_book(a, b, c, d, m, n_sub, book_ref[core_ref[0] * n_sub + m])
        book_out[m] = book
        w, stats = assign(book, feats[SUB_DIM * m : SUB_DIM * (m + 1)])
        w_ref[m] = w
        write_stats(stats_ref, m, n_sub, stats)


def cross_kernel(a, b, c, d, book_ref, w_ref, own_ref, oth_ref, book_out, cross_ref):
    n_sub = w_ref.shape[0]
    parts = []
    for m in range(n_sub):
        book = new_book(a, b, c, d, m, n_sub, book_ref[m])
        book_out[m] = book
        parts.append(dot(book.astype(bf16), w_ref[m]).astype(bf16))
    rebuilt = jnp.concatenate(parts, axis=0)
    n = own_ref.shape[1]
    for p in range(SUB_DEVS // 2):
        mine = jnp.concatenate([own_ref[2 * p], own_ref[2 * p + 1]], axis=1)
        other = jnp.concatenate([oth_ref[2 * p], oth_ref[2 * p + 1]], axis=1)
        part = dot(rebuilt[:, :n], mine) + dot(rebuilt[:, n:], other)
        h, q = divmod(p, 2)
        for t in range(part.shape[0] // 8):
            cross_ref[2 * t + h, :, 256 * q : 256 * (q + 1)] = part[8 * t : 8 * (t + 1)]


def sum_kernel(x_ref, out_ref):
    total = x_ref[0]
    for i in range(1, x_ref.shape[0]):
        total = total + x_ref[i]
    for i in range(out_ref.shape[0]):
        out_ref[i] = total


def columns_kernel(x_ref, v_ref, low_ref):
    for t in range(x_ref.shape[0] // 2):
        v_ref[8 * t : 8 * (t + 1)] = jnp.concatenate([x_ref[2 * t], x_ref[2 * t + 1]], axis=1)
    low = v_ref[...].astype(bf16)
    for i in range(SUB_DEVS):
        low_ref[i] = low


def polar_kernel(core_ref, base_ref, own_ref, oth_ref, vown_ref, voth_ref, out_ref, hi_ref, lo_ref):
    width = vown_ref.shape[1]
    gram = jnp.zeros((width, width), f32)
    for ref in (own_ref, oth_ref):
        cols = ref[...].reshape(-1, width)
        gram = gram + dot(cols, cols, ((0,), (0,)))
    eye = lax.broadcasted_iota(jnp.int32, (128, 128), 0) == lax.broadcasted_iota(jnp.int32, (128, 128), 1)
    diag = jnp.zeros((128, 128), f32)
    for i in range(0, width, 128):
        diag = diag + jnp.where(eye, gram[i : i + 128, i : i + 128], 0.0)
    square = jnp.sum(jnp.sum(diag, axis=0, keepdims=True), axis=1, keepdims=True) + 1e-06
    gram = gram * (1.0 / square)
    hi = gram.astype(bf16)
    hi_ref[...] = hi
    lo_ref[...] = (gram - hi.astype(f32)).astype(bf16)

    def times_gram(v):
        v_hi = v.astype(bf16)
        v_lo = (v - v_hi.astype(f32)).astype(bf16)
        n = v.shape[0]
        both = dot(jnp.concatenate([v_hi, v_lo], axis=0), hi_ref[...])
        return both[:n] + (both[n:] + dot(v_hi, lo_ref[...]))

    def quintic(v):
        image = times_gram(v)
        return Q1 * v + Q3 * image + Q5 * times_gram(image)

    def times_next_gram(v):
        return quintic(times_gram(quintic(v)))

    polar = jnp.concatenate([vown_ref[...], voth_ref[...]], axis=0) * (1.0 / jnp.sqrt(square))
    polar = quintic(polar)
    image = times_next_gram(polar)
    second = times_next_gram(image)
    polar = Q1 * polar + Q3 * image + Q5 * second
    n = out_ref.shape[0]
    pick = lax.broadcasted_iota(jnp.int32, (n, width), 1) == lax.broadcasted_iota(jnp.int32, (n, width), 0) + base_ref[0]
    out = dot(pick.astype(f32), polar, ((1,), (1,)), lax.Precision.HIGHEST)
    out_ref[...] = jnp.where(core_ref[0] == 0, out, pltpu.roll(out, out.shape[1] // 2, 1))


def sum_over_chips(stats):
    x = [permute_rows(stats, lambda i, d=d: i ^ (2 * d)) for d in (1, 2, 3)]
    stats = (stats + x[0]) + (x[1] + x[2])
    z = [permute_rows(stats, lambda i, d=d: i ^ (8 * d)) for d in (1, 2, 3)]
    return stats, z[0], z[1], z[2]


def per_device(embeddings, rotation, codebooks):
    n, _ = embeddings.shape
    width = rotation.shape[0]
    subs, _, codes = codebooks.shape
    n_sub = subs // 2
    half = n_sub * SUB_DIM
    row_index = lax.axis_index("rows")
    core = (row_index % 2).astype(jnp.int32)
    core_arr = core.reshape(1)
    base = (row_index * (width // ROW_DEVS)).astype(jnp.int32).reshape(1)

    e_own = gather_by_exchange(embeddings, "sub", SUB_DEVS)
    keep, send = call(rotate_kernel, (shape((half, n), bf16),) * 2, 1, 2)(core_arr, e_own, rotation)
    recv = other_core(send)
    e_oth = other_core(e_own)

    stats_shape = shape((half + 8, codes), f32)
    stats = call(first_kernel, stats_shape, 1, 3)(core_arr, keep, recv, codebooks)
    sums = sum_over_chips(stats)
    book, weights, stats = call(
        second_kernel,
        (shape((n_sub, SUB_DIM, codes), f32), shape((n_sub, codes, 2 * n), bf16), stats_shape),
        1,
        7,
    )(core_arr, keep, recv, codebooks, *sums)
    sums = sum_over_chips(stats)
    book, cross = call(
        cross_kernel,
        (shape((n_sub, SUB_DIM, codes), f32), shape((16, 8, width // 2), f32)),
        0,
        8,
    )(*sums, book, weights, e_own, e_oth)

    cross = lax.all_to_all(cross, "rows", 0, 0, tiled=True, axis_index_groups=CHIPS)
    copies = call(sum_kernel, shape(cross.shape, f32), 0, 1)(cross)
    cols = lax.all_to_all(copies, "rows", 0, 0, tiled=True, axis_index_groups=CHIPS)
    v_own, low = call(
        columns_kernel, (shape((half, width), f32), shape((SUB_DEVS, half, width), bf16)), 0, 1
    )(cols)
    v_oth = other_core(v_own)
    book_oth = other_core(book)
    c_own = lax.all_to_all(low, "sub", 0, 0, tiled=True)
    c_oth = other_core(c_own)
    new_rotation = call(
        polar_kernel,
        shape((width // ROW_DEVS, 2 * half), f32),
        2,
        4,
        (pltpu.VMEM((width, width), bf16), pltpu.VMEM((width, width), bf16)),
    )(core_arr, base, c_own, c_oth, v_own, v_oth)
    first = core == 0
    books = jnp.concatenate([jnp.where(first, book, book_oth), jnp.where(first, book_oth, book)], axis=0)
    return (books, new_rotation)


def solution(mesh):
    return jax.shard_map(
        per_device,
        mesh=mesh,
        in_specs=(P("rows", "sub"), P(None, "sub"), P("sub", None, None)),
        out_specs=(P("sub", None, None), P("rows", "sub")),
        check_vma=False,
    )
```

```python
import jax
import jax.numpy as jnp
from jax import lax
from jax.experimental import pallas as pl
from jax.experimental.pallas import tpu as pltpu
from jax.sharding import PartitionSpec as P

SUB_DIM = 16
CODES = 256
SOFTNESS = 4.0
PRIOR = 8.0
Q1, Q3, Q5 = 3.4445, -4.775, 2.0315

ROW_DEVS = 32
SUB_DEVS = 8
CHIPS = [[8 * z + 2 * x + c for z in range(4) for x in range(4)] for c in range(2)]

f32 = jnp.float32
bf16 = jnp.bfloat16
VMEM_LIMIT = 48 * 1024 * 1024


def call(kernel, out_shape, n_scalars, n_arrays, scratch=()):
    return pl.pallas_call(
        kernel,
        out_shape=out_shape,
        in_specs=[pl.BlockSpec(memory_space=pltpu.SMEM)] * n_scalars
        + [pl.BlockSpec(memory_space=pltpu.VMEM)] * n_arrays,
        scratch_shapes=list(scratch),
        compiler_params=pltpu.CompilerParams(vmem_limit_bytes=VMEM_LIMIT),
    )


def shape(dims, dtype):
    return jax.ShapeDtypeStruct(dims, dtype)


def dot(a, b, dims=((1,), (0,)), precision=None):
    return lax.dot_general(a, b, (dims, ((), ())), precision=precision, preferred_element_type=f32)


def permute_rows(x, to):
    return lax.ppermute(x, "rows", [(i, to(i)) for i in range(ROW_DEVS)])


def other_core(x):
    return permute_rows(x, lambda i: i ^ 1)


def load_kernel(sub_ref, r_ref, e_ref, book_ref, r_out, e_out, book_out):
    n = e_ref.shape[1]
    for k in range(SUB_DEVS):
        r_out[n * k : n * (k + 1)] = r_ref[pl.ds(pl.multiple_of((sub_ref[0] ^ k) * n, n), n)]
    e_out[...] = e_ref[...]
    book_out[...] = book_ref[...]


def rotate_kernel(place_ref, *refs):
    e_refs, r_ref, keep_ref, send_ref, feats_ref, rot_ref = refs[:SUB_DEVS], *refs[SUB_DEVS:]
    n = e_refs[0].shape[1]
    for k in range(SUB_DEVS):
        feats_ref[:, n * k : n * (k + 1)] = e_refs[k][...]
    rot = dot(feats_ref[...], r_ref[...]).T.astype(bf16)
    for m in range(rot_ref.shape[0]):
        rot_ref[m] = rot[SUB_DIM * m : SUB_DIM * (m + 1)]
    core, x = place_ref[0], place_ref[1]
    for d in range(4):
        keep_ref[d] = rot_ref[4 * core + (x ^ d)]
        send_ref[d] = rot_ref[4 * (1 - core) + (x ^ d)]


def join_kernel(keep_ref, recv_ref, *outs):
    n = keep_ref.shape[2]
    for d, out in enumerate(outs):
        out[:, :n] = keep_ref[d + 1]
        out[:, n:] = recv_ref[d + 1]


def assign(book, feats):
    sq = 0.25 * jnp.sum(book * book, axis=0, keepdims=True)
    sq_a = sq.astype(bf16).astype(f32)
    sq_b = (sq - sq_a).astype(bf16).astype(f32)
    sq_c = (sq - sq_a) - sq_b
    low = book.astype(bf16).astype(f32)
    pad = jnp.zeros((SUB_DIM - 3, book.shape[1]), f32)
    lhs = jnp.concatenate([0.5 * low, -sq_a, -sq_b, -sq_c, pad], axis=0).T.astype(bf16)
    rhs = jnp.concatenate([feats, jnp.ones_like(feats)], axis=0)
    logits = dot(lhs, rhs)
    e = jnp.exp(logits - jnp.max(logits, axis=0, keepdims=True))
    w = (e * (1.0 / jnp.sum(e, axis=0, keepdims=True))).astype(bf16)
    stats = dot(rhs, w, ((1,), (1,)))
    return w, stats


def assign_all(book, f_refs, stats_ref, w_ref=None):
    keep_ref, recv_ref = f_refs[:2]
    total = None
    for d in range(4):
        feats = f_refs[d + 1][...] if d else jnp.concatenate([keep_ref[0], recv_ref[0]], axis=1)
        w, stats = assign(book, feats)
        total = stats if total is None else total + stats
        if w_ref is not None:
            w_ref[d] = w
    stats_ref[...] = total[: stats_ref.shape[0]]


def first_kernel(place_ref, k, r, f1, f2, f3, book_ref, stats_ref):
    assign_all(book_ref[4 * place_ref[0] + place_ref[1]], (k, r, f1, f2, f3), stats_ref)


def new_book(a, b, c, d, book):
    stats = (a[...] + b[...]) + (c[...] + d[...])
    return (stats[:SUB_DIM] + PRIOR * book) / (stats[SUB_DIM : SUB_DIM + 1] + PRIOR)


def second_kernel(place_ref, k, r, f1, f2, f3, book_ref, a, b, c, d, book_out, w_ref, stats_ref):
    book = new_book(a, b, c, d, book_ref[4 * place_ref[0] + place_ref[1]])
    book_out[...] = book
    assign_all(book, (k, r, f1, f2, f3), stats_ref, w_ref)


def rebuild_kernel(a, b, c, d, book_ref, w_ref, book_out, *outs):
    book = new_book(a, b, c, d, book_ref[...])
    n = book_out.shape[2]
    for q in range(book_out.shape[0]):
        for h in range(2):
            book_out[q, 4 * h : 4 * (h + 1)] = book[4 * q : 4 * (q + 1), n * h : n * (h + 1)]
    low = book.astype(bf16)
    for i, out in enumerate(outs):
        out[...] = dot(low, w_ref[i]).astype(bf16)


def cross_kernel(place_ref, x0, x1, x2, x3, own_ref, oth_ref, out_ref, rebuilt_ref):
    for d, x in enumerate((x0, x1, x2, x3)):
        at = pl.multiple_of((place_ref[1] ^ d) * SUB_DIM, SUB_DIM)
        rebuilt_ref[pl.ds(at, SUB_DIM)] = x[...]
    n = own_ref.shape[0]
    width = out_ref.shape[2]
    for h in range(2):
        at = slice(width * h, width * (h + 1))
        part = dot(rebuilt_ref[:, :n], own_ref[:, at]) + dot(rebuilt_ref[:, n:], oth_ref[:, at])
        for t in range(part.shape[0] // 8):
            out_ref[2 * t + h] = part[8 * t : 8 * (t + 1)]


def sum_kernel(z_ref, x_ref, book_ref, out_ref):
    total = x_ref[0]
    for i in range(1, x_ref.shape[0]):
        total = total + x_ref[i]
    both = jnp.concatenate([total, book_ref[z_ref[0]]], axis=1)
    for i in range(out_ref.shape[0]):
        out_ref[i] = both


def columns_kernel(sub_ref, x_ref, v_ref, low_ref):
    n = low_ref.shape[1] // SUB_DEVS
    rows = low_ref.shape[0]
    for k in range(SUB_DEVS):
        at = pl.ds(pl.multiple_of((sub_ref[0] ^ k) * n, n), n)
        h, q = divmod(k, SUB_DEVS // 2)
        block = jnp.concatenate([x_ref[2 * t + h, :, n * q : n * (q + 1)] for t in range(rows // 8)], axis=0)
        v_ref[:rows, at] = block
        low_ref[:, at] = block.astype(bf16)
    for i in range(x_ref.shape[0]):
        u, v = divmod(i, SUB_DEVS)
        v_ref[rows + 8 * u : rows + 8 * (u + 1), n * v : n * (v + 1)] = x_ref[i, :, n * 4 :]


def polar_kernel(place_ref, c0, c1, c2, c3, vown_ref, voth_ref, out_ref, book_out, hi_ref, lo_ref, all_ref, block_ref):
    width = vown_ref.shape[1]
    rows = c0.shape[1]
    core = place_ref[0]
    n = book_out.shape[2] // 2
    for ref, at in ((vown_ref, core), (voth_ref, 1 - core)):
        for i in range(16):
            z, x = divmod(i, 4)
            u, v = divmod(i, SUB_DEVS)
            part = ref[rows + 8 * u : rows + 8 * (u + 1), n * v : n * (v + 1)]
            for h in range(2):
                book_out[4 * at + x, 4 * z : 4 * (z + 1), n * h : n * (h + 1)] = part[4 * h : 4 * (h + 1)]
    cols = jnp.concatenate([c[...].reshape(-1, width) for c in (c0, c1, c2, c3)], axis=0)
    gram = dot(cols, cols, ((0,), (0,)))
    eye = lax.broadcasted_iota(jnp.int32, (n, n), 0) == lax.broadcasted_iota(jnp.int32, (n, n), 1)
    diag = jnp.zeros((n, n), f32)
    for i in range(0, width, n):
        diag = diag + jnp.where(eye, gram[i : i + n, i : i + n], 0.0)
    square = jnp.sum(jnp.sum(diag, axis=0, keepdims=True), axis=1, keepdims=True) + 1e-06
    gram = gram * (1.0 / square)
    hi = gram.astype(bf16)
    hi_ref[...] = hi
    lo_ref[...] = (gram - hi.astype(f32)).astype(bf16)

    def times_gram(v):
        v_hi = v.astype(bf16)
        v_lo = (v - v_hi.astype(f32)).astype(bf16)
        n = v.shape[0]
        both = dot(jnp.concatenate([v_hi, v_lo], axis=0), hi_ref[...])
        return both[:n] + (both[n:] + dot(v_hi, lo_ref[...]))

    def quintic(v):
        image = times_gram(v)
        return Q1 * v + Q3 * image + Q5 * times_gram(image)

    def times_next_gram(v):
        return quintic(times_gram(quintic(v)))

    polar = jnp.concatenate([vown_ref[:rows], voth_ref[:rows]], axis=0) * (1.0 / jnp.sqrt(square))
    polar = quintic(polar)
    image = times_next_gram(polar)
    second = times_next_gram(image)
    all_ref[...] = Q1 * polar + Q3 * image + Q5 * second
    n_out = out_ref.shape[0]
    block, at = place_ref[2] // (n // n_out), place_ref[2] % (n // n_out)
    block_ref[...] = all_ref[:, pl.ds(pl.multiple_of(block * n, n), n)].T
    out = block_ref[pl.ds(pl.multiple_of(at * n_out, n_out), n_out)]
    out_ref[...] = jnp.where(core == 0, out, pltpu.roll(out, rows, 1))


def over_sub(x, k):
    return lax.ppermute(x, "sub", [(i, i ^ k) for i in range(SUB_DEVS)])


def over_y(x):
    return [over_sub(x, 2 * d) for d in (1, 2, 3)]


def mirror_z(x):
    pairs = []
    for z in range(4):
        for j in range(8):
            for s in range(SUB_DEVS):
                pairs.append(((8 * z + j) * SUB_DEVS + s, (8 * (3 - z) + j) * SUB_DEVS + (s ^ 1)))
    return lax.ppermute(x, ("rows", "sub"), pairs)


def over_z(x):
    return [x] + [permute_rows(x, lambda i, d=d: i ^ (8 * d)) for d in (1, 2, 3)]


def over_x(xs):
    return [permute_rows(x, lambda i, d=d: i ^ (2 * d)) for d, x in zip((1, 2, 3), xs)]


def exchange(x, groups):
    return lax.all_to_all(x, "rows", 0, 0, tiled=True, axis_index_groups=groups)


def per_device(embeddings, rotation, codebooks):
    n, n_feat = embeddings.shape
    width = rotation.shape[0]
    subs, _, codes = codebooks.shape
    half = subs * SUB_DIM // 2
    row_index = lax.axis_index("rows").astype(jnp.int32)
    place = jnp.stack([row_index % 2, (row_index // 2) % 4, row_index])
    z = (row_index // 8).reshape(1)
    sub = lax.axis_index("sub").astype(jnp.int32).reshape(1)

    z_block = over_sub(embeddings, 1)
    own_y = over_y(embeddings)
    other_y = over_y(z_block)
    mats, mine, books = call(
        load_kernel, tuple(shape(v.shape, v.dtype) for v in (rotation, embeddings, codebooks)), 1, 3
    )(sub, rotation, embeddings, codebooks)
    blocks = [mine, z_block]
    for a, b in zip(own_y, other_y):
        blocks += [a, b]
    part = shape((4, SUB_DIM, n), bf16)
    keep, send, e_own = call(
        rotate_kernel,
        (part, part, shape((n, width), bf16)),
        1,
        SUB_DEVS + 1,
        (pltpu.VMEM((subs, SUB_DIM, n), bf16),),
    )(place, *blocks, mats)
    recv = other_core(send)
    e_own, recv = lax.optimization_barrier((e_own, recv))
    e_oth = other_core(e_own)
    piece = shape((SUB_DIM, 2 * n), bf16)
    feats = (keep, recv, *over_x(call(join_kernel, (piece,) * 3, 0, 2)(keep, recv)))

    stats_shape = shape((SUB_DIM + 8, codes), f32)
    stats = call(first_kernel, stats_shape, 1, 6)(place, *feats, books)
    book, weights, stats = call(
        second_kernel, (shape((SUB_DIM, codes), f32), shape((4, codes, 2 * n), bf16), stats_shape), 1, 10
    )(place, *feats, books, *over_z(stats))
    book, *rebuilt = call(rebuild_kernel, (shape((4, 8, codes // 2), f32),) + (piece,) * 4, 0, 6)(
        *over_z(stats), book, weights
    )
    cross = call(
        cross_kernel, shape((16, 8, width // 2), f32), 1, 6, (pltpu.VMEM((half, 2 * n), bf16),)
    )(place, rebuilt[0], *over_x(rebuilt[1:]), e_own, e_oth)

    cross = exchange(cross, CHIPS)
    copies = call(sum_kernel, shape((16, 8, width // 2 + codes // 2), f32), 1, 2)(z, cross, book)
    cols = exchange(copies, CHIPS)
    v_own, low = call(
        columns_kernel, (shape((half + SUB_DIM, width), f32), shape((half, width), bf16)), 1, 1
    )(sub, cols)
    v_oth = other_core(v_own)
    z_low = mirror_z(low)
    c_own = jnp.stack([low] + over_y(low))
    c_oth = other_core(c_own)
    z_own = jnp.stack([z_low] + over_y(z_low))
    z_oth = other_core(z_own)
    new_rotation, new_codebooks = call(
        polar_kernel,
        (shape((width // ROW_DEVS, 2 * half), f32), shape(codebooks.shape, f32)),
        1,
        6,
        (
            pltpu.VMEM((width, width), bf16),
            pltpu.VMEM((width, width), bf16),
            pltpu.VMEM((2 * half, width), f32),
            pltpu.VMEM((128, 2 * half), f32),
        ),
    )(place, c_own, c_oth, z_own, z_oth, v_own, v_oth)
    return (new_codebooks, new_rotation)


def solution(mesh):
    return jax.shard_map(
        per_device,
        mesh=mesh,
        in_specs=(P("rows", "sub"), P(None, "sub"), P("sub", None, None)),
        out_specs=(P("sub", None, None), P("rows", "sub")),
        check_vma=False,
    )
```

```python
import jax
import jax.numpy as jnp
from jax import lax
from jax.experimental import pallas as pl
from jax.experimental.pallas import tpu as pltpu
from jax.sharding import PartitionSpec as P

SUB_DIM = 16
CODES = 256
SOFTNESS = 4.0
PRIOR = 8.0
Q1, Q3, Q5 = 3.4445, -4.775, 2.0315

ROW_DEVS = 32
SUB_DEVS = 8

f32 = jnp.float32
bf16 = jnp.bfloat16
VMEM_LIMIT = 48 * 1024 * 1024


def call(kernel, out_shape, n_scalars, n_arrays, scratch=()):
    return pl.pallas_call(
        kernel,
        out_shape=out_shape,
        in_specs=[pl.BlockSpec(memory_space=pltpu.SMEM)] * n_scalars
        + [pl.BlockSpec(memory_space=pltpu.VMEM)] * n_arrays,
        scratch_shapes=list(scratch),
        compiler_params=pltpu.CompilerParams(vmem_limit_bytes=VMEM_LIMIT),
    )


def shape(dims, dtype):
    return jax.ShapeDtypeStruct(dims, dtype)


def dot(a, b, dims=((1,), (0,)), precision=None):
    return lax.dot_general(a, b, (dims, ((), ())), precision=precision, preferred_element_type=f32)


def permute_rows(x, to):
    return lax.ppermute(x, "rows", [(i, to(i)) for i in range(ROW_DEVS)])


def other_core(x):
    return permute_rows(x, lambda i: i ^ 1)


def load_kernel(place_ref, r_ref, e_ref, book_ref, r_out, e_out, book_out):
    n = e_ref.shape[1]
    for k in range(SUB_DEVS):
        r_out[n * k : n * (k + 1)] = r_ref[pl.ds(pl.multiple_of((place_ref[3] ^ k) * n, n), n)]
    e_out[...] = e_ref[...]
    book_out[...] = book_ref[...]


def rotate_kernel(place_ref, *refs):
    e_refs, r_ref, keep_ref, send_ref, feats_ref, rot_ref = refs[:SUB_DEVS], *refs[SUB_DEVS:]
    n = e_refs[0].shape[1]
    for k in range(SUB_DEVS):
        feats_ref[:, n * k : n * (k + 1)] = e_refs[k][...]
    rot = dot(feats_ref[...], r_ref[...]).T.astype(bf16)
    for m in range(rot_ref.shape[0]):
        rot_ref[m] = rot[SUB_DIM * m : SUB_DIM * (m + 1)]
    core, x = place_ref[0], place_ref[1]
    for d in range(4):
        keep_ref[d] = rot_ref[4 * core + (x ^ d)]
        send_ref[d] = rot_ref[4 * (1 - core) + (x ^ d)]


def join_kernel(keep_ref, recv_ref, *outs):
    n = keep_ref.shape[2]
    for d, out in enumerate(outs):
        out[:, :n] = keep_ref[d + 1]
        out[:, n:] = recv_ref[d + 1]


def score_matrix(book):
    sq = 0.25 * jnp.sum(book * book, axis=0, keepdims=True)
    sq_a = sq.astype(bf16).astype(f32)
    sq_b = (sq - sq_a).astype(bf16).astype(f32)
    sq_c = (sq - sq_a) - sq_b
    low = book.astype(bf16).astype(f32)
    pad = jnp.zeros((SUB_DIM - 3, book.shape[1]), f32)
    return jnp.concatenate([0.5 * low, -sq_a, -sq_b, -sq_c, pad], axis=0).T.astype(bf16)


def assign(lhs, feats):
    rhs = jnp.concatenate([feats, jnp.ones_like(feats)], axis=0)
    logits = dot(lhs, rhs)
    e = jnp.exp(logits - jnp.max(logits, axis=0, keepdims=True))
    w = (e * (1.0 / jnp.sum(e, axis=0, keepdims=True))).astype(bf16)
    return w, dot(rhs, w, ((1,), (1,)))


def assign_all(book, f_refs, stats_ref, w_ref=None):
    keep_ref, recv_ref = f_refs[:2]
    n = keep_ref.shape[2]
    lhs = score_matrix(book)
    total = None
    for d in range(4):
        for h in range(2):
            at = slice(n * h, n * (h + 1))
            feats = f_refs[d + 1][:, at] if d else f_refs[h][0]
            w, stats = assign(lhs, feats)
            total = stats if total is None else total + stats
            if w_ref is not None:
                w_ref[d, :, at] = w
    stats_ref[...] = total[: stats_ref.shape[0]]


def first_kernel(place_ref, k, r, f1, f2, f3, book_ref, stats_ref):
    assign_all(book_ref[4 * place_ref[0] + place_ref[1]], (k, r, f1, f2, f3), stats_ref)


def new_book(a, b, c, d, book):
    stats = (a[...] + b[...]) + (c[...] + d[...])
    return (stats[:SUB_DIM] + PRIOR * book) / (stats[SUB_DIM : SUB_DIM + 1] + PRIOR)


def second_kernel(place_ref, k, r, f1, f2, f3, book_ref, a, b, c, d, book_out, w_ref, stats_ref):
    book = new_book(a, b, c, d, book_ref[4 * place_ref[0] + place_ref[1]])
    book_out[...] = book
    assign_all(book, (k, r, f1, f2, f3), stats_ref, w_ref)


def rebuild_kernel(a, b, c, d, book_ref, w_ref, book_out, *outs):
    book = new_book(a, b, c, d, book_ref[...])
    book_out[...] = book
    low = book.astype(bf16)
    for i, out in enumerate(outs):
        out[...] = dot(low, w_ref[i]).astype(bf16)


def cross_kernel(x0, x1, x2, x3, own_ref, oth_ref, *outs):
    rebuilt = jnp.concatenate([x0[...], x1[...], x2[...], x3[...]], axis=0)
    n = own_ref.shape[0]
    part = dot(rebuilt[:, :n], own_ref[...]) + dot(rebuilt[:, n:], oth_ref[...])
    for i, out in enumerate(outs):
        out[...] = part[SUB_DIM * i : SUB_DIM * (i + 1)]


def sum_kernel(a, b, c, d, book_ref, out_ref):
    n = a.shape[1]
    out_ref[:, :n] = (a[...] + b[...]) + (c[...] + d[...])
    out_ref[:, n:] = book_ref[...]


def columns_kernel(place_ref, x0, x1, x2, x3, v_ref, low_ref):
    width = low_ref.shape[1]
    n = width // SUB_DEVS
    for d, x in enumerate((x0, x1, x2, x3)):
        rows = pl.ds(pl.multiple_of((place_ref[1] ^ d) * SUB_DIM, SUB_DIM), SUB_DIM)
        for k in range(SUB_DEVS):
            at = pl.ds(pl.multiple_of((place_ref[3] ^ k) * n, n), n)
            block = x[:, n * k : n * (k + 1)]
            v_ref[rows, at] = block
            low_ref[rows, at] = block.astype(bf16)
        v_ref[rows, width:] = x[:, width:]


def polar_kernel(
    place_ref, c0, c1, c2, c3, v_ref, book_ref, keep_ref, send_ref, book_out, hi_ref, lo_ref, all_ref, block_ref
):
    rows, width = all_ref.shape
    core = place_ref[0]
    n = block_ref.shape[0]
    for x in range(4):
        at = slice(SUB_DIM * x, SUB_DIM * (x + 1))
        book_out[4 * core + x] = v_ref[at, width:]
        book_out[4 * (1 - core) + x] = book_ref[at]
    cols = jnp.concatenate([c[...].reshape(-1, width) for c in (c0, c1, c2, c3)], axis=0)
    gram = dot(cols, cols, ((0,), (0,)))
    eye = lax.broadcasted_iota(jnp.int32, (n, n), 0) == lax.broadcasted_iota(jnp.int32, (n, n), 1)
    diag = jnp.zeros((n, n), f32)
    for i in range(0, width, n):
        diag = diag + jnp.where(eye, gram[i : i + n, i : i + n], 0.0)
    square = jnp.sum(jnp.sum(diag, axis=0, keepdims=True), axis=1, keepdims=True) + 1e-06
    gram = gram * (1.0 / square)
    hi = gram.astype(bf16)
    hi_ref[...] = hi
    lo_ref[...] = (gram - hi.astype(f32)).astype(bf16)

    def times_gram(v):
        v_hi = v.astype(bf16)
        v_lo = (v - v_hi.astype(f32)).astype(bf16)
        n = v.shape[0]
        both = dot(jnp.concatenate([v_hi, v_lo], axis=0), hi_ref[...])
        return both[:n] + (both[n:] + dot(v_hi, lo_ref[...]))

    def quintic(v):
        image = times_gram(v)
        return Q1 * v + Q3 * image + Q5 * times_gram(image)

    def times_next_gram(v):
        return quintic(times_gram(quintic(v)))

    polar = v_ref[:, :width] * (1.0 / jnp.sqrt(square))
    polar = quintic(polar)
    image = times_next_gram(polar)
    second = times_next_gram(image)
    all_ref[...] = Q1 * polar + Q3 * image + Q5 * second
    n_out = keep_ref.shape[0]
    per_block = n // n_out
    block_ref[...] = all_ref[:, pl.ds(pl.multiple_of(place_ref[2] // per_block * n, n), n)].T
    at = place_ref[2] % per_block
    keep_ref[...] = block_ref[pl.ds(pl.multiple_of(at * n_out, n_out), n_out)]
    send_ref[...] = block_ref[pl.ds(pl.multiple_of((at ^ 1) * n_out, n_out), n_out)]


def over_sub(x, k):
    return lax.ppermute(x, "sub", [(i, i ^ k) for i in range(SUB_DEVS)])


def over_y(x):
    return [over_sub(x, 2 * d) for d in (1, 2, 3)]


def over_sub_mirrored(x, k):
    pairs = []
    for z in range(4):
        for j in range(8):
            for s in range(SUB_DEVS):
                pairs.append(((8 * z + j) * SUB_DEVS + s, (8 * (3 - z) + j) * SUB_DEVS + (s ^ k)))
    return lax.ppermute(x, ("rows", "sub"), pairs)


def others_over_sub(x, across):
    partner = across(x, 1)
    y = over_y(x)
    far = across(x, 5)
    return [partner, y[0], over_sub(partner, 2), y[1], far, y[2], over_sub(partner, 6)]


def over_z(x):
    return [x] + [permute_rows(x, lambda i, d=d: i ^ (8 * d)) for d in (1, 2, 3)]


def over_x(xs):
    return [permute_rows(x, lambda i, d=d: i ^ (2 * d)) for d, x in zip((1, 2, 3), xs)]


def per_device(embeddings, rotation, codebooks):
    n, n_feat = embeddings.shape
    width = rotation.shape[0]
    subs, _, codes = codebooks.shape
    half = subs * SUB_DIM // 2
    row_index = lax.axis_index("rows").astype(jnp.int32)
    sub = lax.axis_index("sub").astype(jnp.int32)
    core = row_index % 2
    place = jnp.stack([core, (row_index // 2) % 4, row_index, sub])

    others = others_over_sub(embeddings, over_sub)
    mats, mine, books = call(
        load_kernel, tuple(shape(v.shape, v.dtype) for v in (rotation, embeddings, codebooks)), 1, 3
    )(place, rotation, embeddings, codebooks)
    part = shape((4, SUB_DIM, n), bf16)
    keep, send, e_own = call(
        rotate_kernel,
        (part, part, shape((n, width), bf16)),
        1,
        SUB_DEVS + 1,
        (pltpu.VMEM((subs, SUB_DIM, n), bf16),),
    )(place, mine, *others, mats)
    recv = other_core(send)
    e_own, recv = lax.optimization_barrier((e_own, recv))
    e_oth = other_core(e_own)
    piece = shape((SUB_DIM, 2 * n), bf16)
    feats = (keep, recv, *over_x(call(join_kernel, (piece,) * 3, 0, 2)(keep, recv)))

    stats_shape = shape((SUB_DIM + 8, codes), f32)
    stats = call(first_kernel, stats_shape, 1, 6)(place, *feats, books)
    book, weights, stats = call(
        second_kernel, (shape((SUB_DIM, codes), f32), shape((4, codes, 2 * n), bf16), stats_shape), 1, 10
    )(place, *feats, books, *over_z(stats))
    book, *rebuilt = call(rebuild_kernel, (shape((SUB_DIM, codes), f32),) + (piece,) * 4, 0, 6)(
        *over_z(stats), book, weights
    )
    chunk = shape((SUB_DIM, width), f32)
    cross = call(cross_kernel, (chunk,) * 4, 0, 6)(rebuilt[0], *over_x(rebuilt[1:]), e_own, e_oth)
    got = over_x(cross[1:])
    mine = (cross[0] + got[0]) + (got[1] + got[2])
    mine = call(sum_kernel, shape((SUB_DIM, width + codes), f32), 0, 5)(*over_z(mine), book)
    v_own, low = call(
        columns_kernel, (shape((half, width + codes), f32), shape((half, width), bf16)), 1, 4
    )(place, mine, *over_x([mine] * 3))
    book_oth = other_core(v_own[:, width:])
    partner = over_sub_mirrored(low, 1)
    c_own = jnp.stack([low] + over_y(low))
    c_oth = other_core(c_own)
    z_own = jnp.stack([partner] + over_y(partner))
    z_oth = other_core(z_own)
    piece = shape((width // ROW_DEVS, half), f32)
    keep, send, new_codebooks = call(
        polar_kernel,
        (piece, piece, shape(codebooks.shape, f32)),
        1,
        6,
        (
            pltpu.VMEM((width, width), bf16),
            pltpu.VMEM((width, width), bf16),
            pltpu.VMEM((half, width), f32),
            pltpu.VMEM((128, half), f32),
        ),
    )(place, c_own, c_oth, z_own, z_oth, v_own, book_oth)
    recv = other_core(send)
    new_rotation = jnp.where(core == 0, jnp.concatenate([keep, recv], 1), jnp.concatenate([recv, keep], 1))
    return (new_codebooks, new_rotation)


def solution(mesh):
    return jax.shard_map(
        per_device,
        mesh=mesh,
        in_specs=(P("rows", "sub"), P(None, "sub"), P("sub", None, None)),
        out_specs=(P("sub", None, None), P("rows", "sub")),
        check_vma=False,
    )
```

```python
import jax
import jax.numpy as jnp
from jax import lax
from jax.experimental import pallas as pl
from jax.experimental.pallas import tpu as pltpu
from jax.sharding import PartitionSpec as P

SUB_DIM = 16
CODES = 256
SOFTNESS = 4.0
PRIOR = 8.0
Q1, Q3, Q5 = 3.4445, -4.775, 2.0315

ROW_DEVS = 32
SUB_DEVS = 8
ORDER = (0, 2, 3, 1)
BLOCKS = (0, 1, 4, 5, 6, 7, 2, 3)

f32 = jnp.float32
bf16 = jnp.bfloat16
VMEM_LIMIT = 48 * 1024 * 1024


def call(kernel, out_shape, n_scalars, n_arrays, scratch=()):
    return pl.pallas_call(
        kernel,
        out_shape=out_shape,
        in_specs=[pl.BlockSpec(memory_space=pltpu.SMEM)] * n_scalars
        + [pl.BlockSpec(memory_space=pltpu.VMEM)] * n_arrays,
        scratch_shapes=list(scratch),
        compiler_params=pltpu.CompilerParams(vmem_limit_bytes=VMEM_LIMIT),
    )


def shape(dims, dtype):
    return jax.ShapeDtypeStruct(dims, dtype)


def dot(a, b, dims=((1,), (0,)), precision=None):
    return lax.dot_general(a, b, (dims, ((), ())), precision=precision, preferred_element_type=f32)


def permute_rows(x, to):
    return lax.ppermute(x, "rows", [(i, to(i)) for i in range(ROW_DEVS)])


def other_core(x):
    return permute_rows(x, lambda i: i ^ 1)


def load_kernel(place_ref, r_ref, e_ref, book_ref, r_out, e_out, book_out):
    n = e_ref.shape[1]
    for k in range(SUB_DEVS):
        r_out[n * k : n * (k + 1)] = r_ref[pl.ds(pl.multiple_of((place_ref[3] ^ BLOCKS[k]) * n, n), n)]
    e_out[...] = e_ref[...]
    book_out[...] = book_ref[...]


def rotate_kernel(place_ref, *refs):
    e_refs, r_ref, keep_ref, send_ref, feats_ref, rot_ref = refs[:SUB_DEVS], *refs[SUB_DEVS:]
    n = e_refs[0].shape[1]
    for k in range(SUB_DEVS):
        feats_ref[:, n * k : n * (k + 1)] = e_refs[k][...]
    rot = dot(feats_ref[...], r_ref[...]).T.astype(bf16)
    for m in range(rot_ref.shape[0]):
        rot_ref[m] = rot[SUB_DIM * m : SUB_DIM * (m + 1)]
    core, x = place_ref[0], place_ref[1]
    for j in range(4):
        keep_ref[j] = rot_ref[4 * core + (x ^ ORDER[j])]
        send_ref[j] = rot_ref[4 * (1 - core) + (x ^ ORDER[j])]


def join_kernel(keep_ref, recv_ref, *outs):
    n = keep_ref.shape[2]
    for d, out in enumerate(outs):
        out[:, :n] = keep_ref[d + 1]
        out[:, n:] = recv_ref[d + 1]


def score_matrix(book):
    sq = 0.25 * jnp.sum(book * book, axis=0, keepdims=True)
    sq_a = sq.astype(bf16).astype(f32)
    sq_b = (sq - sq_a).astype(bf16).astype(f32)
    sq_c = (sq - sq_a) - sq_b
    low = book.astype(bf16).astype(f32)
    pad = jnp.zeros((SUB_DIM - 3, book.shape[1]), f32)
    return jnp.concatenate([0.5 * low, -sq_a, -sq_b, -sq_c, pad], axis=0).T.astype(bf16)


def assign(lhs, feats):
    rhs = jnp.concatenate([feats, jnp.ones_like(feats)], axis=0)
    logits = dot(lhs, rhs)
    e = jnp.exp(logits - jnp.max(logits, axis=0, keepdims=True))
    w = (e * (1.0 / jnp.sum(e, axis=0, keepdims=True))).astype(bf16)
    return w, dot(rhs, w, ((1,), (1,)))


def assign_all(book, f_refs, stats_ref, w_ref=None):
    keep_ref, recv_ref = f_refs[:2]
    n = keep_ref.shape[2]
    lhs = score_matrix(book)
    total = None
    for d in range(4):
        for h in range(2):
            at = slice(n * h, n * (h + 1))
            feats = f_refs[d + 1][:, at] if d else f_refs[h][0]
            w, stats = assign(lhs, feats)
            total = stats if total is None else total + stats
            if w_ref is not None:
                w_ref[d, :, at] = w
    stats_ref[...] = total[: stats_ref.shape[0]]


def first_kernel(place_ref, k, r, f1, f2, f3, book_ref, stats_ref):
    assign_all(book_ref[4 * place_ref[0] + place_ref[1]], (k, r, f1, f2, f3), stats_ref)


def new_book(a, b, c, d, book):
    stats = (a[...] + b[...]) + (c[...] + d[...])
    return (stats[:SUB_DIM] + PRIOR * book) / (stats[SUB_DIM : SUB_DIM + 1] + PRIOR)


def second_kernel(place_ref, k, r, f1, f2, f3, book_ref, a, b, c, d, book_out, w_ref, stats_ref):
    book = new_book(a, b, c, d, book_ref[4 * place_ref[0] + place_ref[1]])
    book_out[...] = book
    assign_all(book, (k, r, f1, f2, f3), stats_ref, w_ref)


def rebuild_kernel(a, b, c, d, book_ref, w_ref, book_out, *outs):
    book = new_book(a, b, c, d, book_ref[...])
    book_out[...] = book
    low = book.astype(bf16)
    for i, out in enumerate(outs):
        out[...] = dot(low, w_ref[i]).astype(bf16)


def cross_kernel(x0, x1, x2, x3, own_ref, oth_ref, *outs):
    rebuilt = jnp.concatenate([x0[...], x1[...], x2[...], x3[...]], axis=0)
    n = own_ref.shape[0]
    part = dot(rebuilt[:, :n], own_ref[...]) + dot(rebuilt[:, n:], oth_ref[...])
    for i, out in enumerate(outs):
        out[...] = part[SUB_DIM * i : SUB_DIM * (i + 1)]


def sum_kernel(a, b, c, d, book_ref, out_ref):
    n = a.shape[1]
    out_ref[:, :n] = (a[...] + b[...]) + (c[...] + d[...])
    out_ref[:, n:] = book_ref[...]


def columns_kernel(place_ref, x0, x1, x2, x3, v_ref, low_ref):
    width = low_ref.shape[1]
    n = width // SUB_DEVS
    for d, x in enumerate((x0, x1, x2, x3)):
        rows = pl.ds(pl.multiple_of((place_ref[1] ^ ORDER[d]) * SUB_DIM, SUB_DIM), SUB_DIM)
        for k in range(SUB_DEVS):
            at = pl.ds(pl.multiple_of((place_ref[3] ^ BLOCKS[k]) * n, n), n)
            block = x[:, n * k : n * (k + 1)]
            v_ref[rows, at] = block
            low_ref[rows, at] = block.astype(bf16)
        v_ref[rows, width:] = x[:, width:]


def pack_kernel(*refs):
    for i, ref in enumerate(refs[:-1]):
        refs[-1][i] = ref[...]


def pack(xs):
    return call(pack_kernel, shape((len(xs),) + xs[0].shape, xs[0].dtype), 0, len(xs))(*xs)


def polar_kernel(
    place_ref, c0, c1, c2, c3, v_ref, book_ref, keep_ref, send_ref, book_out, parts_ref, all_ref, block_ref
):
    rows, width = all_ref.shape
    core = place_ref[0]
    n = block_ref.shape[0]
    for x in range(4):
        at = slice(SUB_DIM * x, SUB_DIM * (x + 1))
        book_out[4 * core + x] = v_ref[at, width:]
        book_out[4 * (1 - core) + x] = book_ref[at]
    cols = jnp.concatenate([c[...].reshape(-1, width) for c in (c0, c1, c2, c3)], axis=0)
    gram = dot(cols.T, cols)
    eye = lax.broadcasted_iota(jnp.int32, (n, n), 0) == lax.broadcasted_iota(jnp.int32, (n, n), 1)
    diag = jnp.zeros((n, n), f32)
    for i in range(0, width, n):
        diag = diag + jnp.where(eye, gram[i : i + n, i : i + n], 0.0)
    square = jnp.sum(jnp.sum(diag, axis=0, keepdims=True), axis=1, keepdims=True) + 1e-06
    gram = gram * (1.0 / square)
    hi = gram.astype(bf16)
    parts_ref[:, :width] = hi
    parts_ref[:, width:] = (gram - hi.astype(f32)).astype(bf16)

    def times_gram(v):
        v_hi = v.astype(bf16)
        v_lo = (v - v_hi.astype(f32)).astype(bf16)
        m = v.shape[0]
        out = dot(jnp.concatenate([v_hi, v_lo], axis=0), parts_ref[...])
        return out[:m, :width] + (out[m:, :width] + out[:m, width:])

    def quintic(v):
        image = times_gram(v)
        return Q1 * v + Q3 * image + Q5 * times_gram(image)

    def times_next_gram(v):
        return quintic(times_gram(quintic(v)))

    polar = v_ref[:, :width] * (1.0 / jnp.sqrt(square))
    polar = quintic(polar)
    image = times_next_gram(polar)
    second = times_next_gram(image)
    all_ref[...] = Q1 * polar + Q3 * image + Q5 * second
    n_out = keep_ref.shape[0]
    per_block = n // n_out
    block_ref[...] = all_ref[:, pl.ds(pl.multiple_of(place_ref[2] // per_block * n, n), n)].T
    at = place_ref[2] % per_block
    keep_ref[...] = block_ref[pl.ds(pl.multiple_of(at * n_out, n_out), n_out)]
    send_ref[...] = block_ref[pl.ds(pl.multiple_of((at ^ 1) * n_out, n_out), n_out)]


def over_sub(x, k):
    return lax.ppermute(x, "sub", [(i, i ^ k) for i in range(SUB_DEVS)])


def over_y(x):
    return [over_sub(x, 2 * d) for d in ORDER[1:]]


def over_sub_mirrored(x, k):
    pairs = []
    for z in range(4):
        for j in range(8):
            for s in range(SUB_DEVS):
                pairs.append(((8 * z + j) * SUB_DEVS + s, (8 * (3 - z) + j) * SUB_DEVS + (s ^ k)))
    return lax.ppermute(x, ("rows", "sub"), pairs)


def others_over_sub(x, across):
    partner = across(x, 1)
    y = over_y(x)
    far = across(x, 5)
    return [partner, y[0], far, y[1], over_sub(partner, 6), y[2], over_sub(partner, 2)]


def over_z(x):
    return [x] + [permute_rows(x, lambda i, d=d: i ^ (8 * d)) for d in ORDER[1:]]


def over_x(xs):
    return [permute_rows(x, lambda i, d=d: i ^ (2 * d)) for d, x in zip(ORDER[1:], xs)]


def per_device(embeddings, rotation, codebooks):
    n, n_feat = embeddings.shape
    width = rotation.shape[0]
    subs, _, codes = codebooks.shape
    half = subs * SUB_DIM // 2
    row_index = lax.axis_index("rows").astype(jnp.int32)
    sub = lax.axis_index("sub").astype(jnp.int32)
    core = row_index % 2
    place = jnp.stack([core, (row_index // 2) % 4, row_index, sub])

    others = others_over_sub(embeddings, over_sub)
    mats, mine, books = call(
        load_kernel, tuple(shape(v.shape, v.dtype) for v in (rotation, embeddings, codebooks)), 1, 3
    )(place, rotation, embeddings, codebooks)
    part = shape((4, SUB_DIM, n), bf16)
    keep, send, e_own = call(
        rotate_kernel,
        (part, part, shape((n, width), bf16)),
        1,
        SUB_DEVS + 1,
        (pltpu.VMEM((subs, SUB_DIM, n), bf16),),
    )(place, mine, *others, mats)
    recv = other_core(send)
    e_own, recv = lax.optimization_barrier((e_own, recv))
    e_oth = other_core(e_own)
    piece = shape((SUB_DIM, 2 * n), bf16)
    feats = (keep, recv, *over_x(call(join_kernel, (piece,) * 3, 0, 2)(keep, recv)))

    stats_shape = shape((SUB_DIM + 8, codes), f32)
    stats = call(first_kernel, stats_shape, 1, 6)(place, *feats, books)
    book, weights, stats = call(
        second_kernel, (shape((SUB_DIM, codes), f32), shape((4, codes, 2 * n), bf16), stats_shape), 1, 10
    )(place, *feats, books, *over_z(stats))
    book, *rebuilt = call(rebuild_kernel, (shape((SUB_DIM, codes), f32),) + (piece,) * 4, 0, 6)(
        *over_z(stats), book, weights
    )
    chunk = shape((SUB_DIM, width), f32)
    cross = call(cross_kernel, (chunk,) * 4, 0, 6)(rebuilt[0], *over_x(rebuilt[1:]), e_own, e_oth)
    got = over_x(cross[1:])
    mine = (cross[0] + got[0]) + (got[1] + got[2])
    mine = call(sum_kernel, shape((SUB_DIM, width + codes), f32), 0, 5)(*over_z(mine), book)
    v_own, low = call(
        columns_kernel, (shape((half, width + codes), f32), shape((half, width), bf16)), 1, 4
    )(place, mine, *over_x([mine] * 3))
    book_oth = other_core(v_own[:, width:])
    partner = over_sub_mirrored(low, 1)
    c_own = pack([low] + over_y(low))
    c_oth = other_core(c_own)
    z_own = pack([partner] + over_y(partner))
    z_oth = other_core(z_own)
    piece = shape((width // ROW_DEVS, half), f32)
    keep, send, new_codebooks = call(
        polar_kernel,
        (piece, piece, shape(codebooks.shape, f32)),
        1,
        6,
        (
            pltpu.VMEM((width, 2 * width), bf16),
            pltpu.VMEM((half, width), f32),
            pltpu.VMEM((128, half), f32),
        ),
    )(place, c_own, c_oth, z_own, z_oth, v_own, book_oth)
    recv = other_core(send)
    new_rotation = jnp.where(core == 0, jnp.concatenate([keep, recv], 1), jnp.concatenate([recv, keep], 1))
    return (new_codebooks, new_rotation)


def solution(mesh):
    return jax.shard_map(
        per_device,
        mesh=mesh,
        in_specs=(P("rows", "sub"), P(None, "sub"), P("sub", None, None)),
        out_specs=(P("sub", None, None), P("rows", "sub")),
        check_vma=False,
    )
```

```python
import jax
import jax.numpy as jnp
from jax import lax
from jax.experimental import pallas as pl
from jax.experimental.pallas import tpu as pltpu
from jax.sharding import PartitionSpec as P

SUB_DIM = 16
CODES = 256
SOFTNESS = 4.0
PRIOR = 8.0
Q1, Q3, Q5 = 3.4445, -4.775, 2.0315

ROW_DEVS = 32
SUB_DEVS = 8
ORDER = (0, 2, 3, 1)
BLOCKS = (0, 1, 4, 5, 6, 7, 2, 3)

f32 = jnp.float32
bf16 = jnp.bfloat16
VMEM_LIMIT = 48 * 1024 * 1024


def call(kernel, out_shape, n_scalars, n_arrays, scratch=()):
    return pl.pallas_call(
        kernel,
        out_shape=out_shape,
        in_specs=[pl.BlockSpec(memory_space=pltpu.SMEM)] * n_scalars
        + [pl.BlockSpec(memory_space=pltpu.VMEM)] * n_arrays,
        scratch_shapes=list(scratch),
        compiler_params=pltpu.CompilerParams(vmem_limit_bytes=VMEM_LIMIT),
    )


def shape(dims, dtype):
    return jax.ShapeDtypeStruct(dims, dtype)


def dot(a, b, dims=((1,), (0,)), precision=None):
    return lax.dot_general(a, b, (dims, ((), ())), precision=precision, preferred_element_type=f32)


def permute_rows(x, to):
    return lax.ppermute(x, "rows", [(i, to(i)) for i in range(ROW_DEVS)])


def other_core(x):
    return permute_rows(x, lambda i: i ^ 1)


def load_kernel(place_ref, r_ref, e_ref, book_ref, r_out, e_out, book_out, scores_out):
    n = e_ref.shape[1]
    for k in range(SUB_DEVS):
        r_out[n * k : n * (k + 1)] = r_ref[pl.ds(pl.multiple_of((place_ref[3] ^ BLOCKS[k]) * n, n), n)]
    e_out[...] = e_ref[...]
    book = book_ref[4 * place_ref[0] + place_ref[1]]
    book_out[...] = book
    scores_out[...] = score_matrix(book)


def rotate_kernel(place_ref, *refs):
    e_refs, r_ref, keep_ref, send_ref, feats_ref, rot_ref = refs[:SUB_DEVS], *refs[SUB_DEVS:]
    n = e_refs[0].shape[1]
    for k in range(SUB_DEVS):
        feats_ref[:, n * k : n * (k + 1)] = e_refs[k][...]
    rot = dot(feats_ref[...], r_ref[...]).T.astype(bf16)
    for m in range(rot_ref.shape[0]):
        rot_ref[m] = rot[SUB_DIM * m : SUB_DIM * (m + 1)]
    core, x = place_ref[0], place_ref[1]
    for j in range(4):
        keep_ref[j] = rot_ref[4 * core + (x ^ ORDER[j])]
        send_ref[j] = rot_ref[4 * (1 - core) + (x ^ ORDER[j])]


def join_kernel(keep_ref, recv_ref, *outs):
    n = keep_ref.shape[2]
    for d, out in enumerate(outs):
        out[:, :n] = keep_ref[d + 1]
        out[:, n:] = recv_ref[d + 1]


def score_matrix(book):
    sq = 0.25 * jnp.sum(book * book, axis=0, keepdims=True)
    sq_a = sq.astype(bf16).astype(f32)
    sq_b = (sq - sq_a).astype(bf16).astype(f32)
    sq_c = (sq - sq_a) - sq_b
    low = book.astype(bf16).astype(f32)
    pad = jnp.zeros((SUB_DIM - 3, book.shape[1]), f32)
    return jnp.concatenate([0.5 * low, -sq_a, -sq_b, -sq_c, pad], axis=0).T.astype(bf16)


def assign(lhs, feats):
    rhs = jnp.concatenate([feats, jnp.ones_like(feats)], axis=0)
    logits = dot(lhs, rhs)
    e = jnp.exp(logits - jnp.max(logits, axis=0, keepdims=True))
    w = (e * (1.0 / jnp.sum(e, axis=0, keepdims=True))).astype(bf16)
    return w, dot(rhs, w, ((1,), (1,)))


def assign_all(lhs, f_refs, stats_ref, w_ref=None):
    keep_ref, recv_ref = f_refs[:2]
    n = keep_ref.shape[2]
    total = None
    for d in range(4):
        for h in range(2):
            at = slice(n * h, n * (h + 1))
            feats = f_refs[d + 1][:, at] if d else f_refs[h][0]
            w, stats = assign(lhs, feats)
            total = stats if total is None else total + stats
            if w_ref is not None:
                w_ref[d, :, at] = w
    stats_ref[...] = total[: stats_ref.shape[0]]


def first_kernel(k, r, f1, f2, f3, scores_ref, stats_ref):
    assign_all(scores_ref[...], (k, r, f1, f2, f3), stats_ref)


def new_book(a, b, c, d, book):
    stats = (a[...] + b[...]) + (c[...] + d[...])
    return (stats[:SUB_DIM] + PRIOR * book) / (stats[SUB_DIM : SUB_DIM + 1] + PRIOR)


def second_kernel(k, r, f1, f2, f3, book_ref, a, b, c, d, book_out, w_ref, stats_ref):
    book = new_book(a, b, c, d, book_ref[...])
    book_out[...] = book
    assign_all(score_matrix(book), (k, r, f1, f2, f3), stats_ref, w_ref)


def rebuild_kernel(a, b, c, d, book_ref, w_ref, book_out, *outs):
    book = new_book(a, b, c, d, book_ref[...])
    book_out[...] = book
    low = book.astype(bf16)
    for i, out in enumerate(outs):
        out[...] = dot(low, w_ref[i]).astype(bf16)


def cross_kernel(x0, x1, x2, x3, own_ref, oth_ref, *outs):
    rebuilt = jnp.concatenate([x0[...], x1[...], x2[...], x3[...]], axis=0)
    n = own_ref.shape[0]
    part = dot(rebuilt[:, :n], own_ref[...]) + dot(rebuilt[:, n:], oth_ref[...])
    for i, out in enumerate(outs):
        out[...] = part[SUB_DIM * i : SUB_DIM * (i + 1)]


def sum_kernel(a, b, c, d, book_ref, out_ref):
    n = a.shape[1]
    out_ref[:, :n] = (a[...] + b[...]) + (c[...] + d[...])
    out_ref[:, n:] = book_ref[...]


def columns_kernel(place_ref, x0, x1, x2, x3, v_ref, low_ref):
    width = low_ref.shape[1]
    n = width // SUB_DEVS
    for d, x in enumerate((x0, x1, x2, x3)):
        rows = pl.ds(pl.multiple_of((place_ref[1] ^ ORDER[d]) * SUB_DIM, SUB_DIM), SUB_DIM)
        for k in range(SUB_DEVS):
            at = pl.ds(pl.multiple_of((place_ref[3] ^ BLOCKS[k]) * n, n), n)
            block = x[:, n * k : n * (k + 1)]
            v_ref[rows, at] = block
            low_ref[rows, at] = block.astype(bf16)
        v_ref[rows, width:] = x[:, width:]


def pack_kernel(*refs):
    for i, ref in enumerate(refs[:-1]):
        refs[-1][i] = ref[...]


def pack(xs):
    return call(pack_kernel, shape((len(xs),) + xs[0].shape, xs[0].dtype), 0, len(xs))(*xs)


def polar_kernel(
    place_ref, c0, c1, c2, c3, v_ref, book_ref, keep_ref, send_ref, book_out, parts_ref, all_ref, block_ref
):
    rows, width = all_ref.shape
    core = place_ref[0]
    n = block_ref.shape[0]
    for x in range(4):
        at = slice(SUB_DIM * x, SUB_DIM * (x + 1))
        book_out[4 * core + x] = v_ref[at, width:]
        book_out[4 * (1 - core) + x] = book_ref[at]
    cols = jnp.concatenate([c[...].reshape(-1, width) for c in (c0, c1, c2, c3)], axis=0)
    gram = dot(cols.T, cols)
    eye = lax.broadcasted_iota(jnp.int32, (n, n), 0) == lax.broadcasted_iota(jnp.int32, (n, n), 1)
    diag = jnp.zeros((n, n), f32)
    for i in range(0, width, n):
        diag = diag + jnp.where(eye, gram[i : i + n, i : i + n], 0.0)
    square = jnp.sum(jnp.sum(diag, axis=0, keepdims=True), axis=1, keepdims=True) + 1e-06
    gram = gram * (1.0 / square)
    hi = gram.astype(bf16)
    parts_ref[:, :width] = hi
    parts_ref[:, width:] = (gram - hi.astype(f32)).astype(bf16)

    def times_gram(v):
        v_hi = v.astype(bf16)
        v_lo = (v - v_hi.astype(f32)).astype(bf16)
        m = v.shape[0]
        out = dot(jnp.concatenate([v_hi, v_lo], axis=0), parts_ref[...])
        return out[:m, :width] + (out[m:, :width] + out[:m, width:])

    def quintic(v):
        image = times_gram(v)
        return Q1 * v + Q3 * image + Q5 * times_gram(image)

    def times_next_gram(v):
        return quintic(times_gram(quintic(v)))

    polar = v_ref[:, :width] * (1.0 / jnp.sqrt(square))
    polar = quintic(polar)
    image = times_next_gram(polar)
    second = times_next_gram(image)
    all_ref[...] = Q1 * polar + Q3 * image + Q5 * second
    n_out = keep_ref.shape[0]
    per_block = n // n_out
    block_ref[...] = all_ref[:, pl.ds(pl.multiple_of(place_ref[2] // per_block * n, n), n)].T
    at = place_ref[2] % per_block
    keep_ref[...] = block_ref[pl.ds(pl.multiple_of(at * n_out, n_out), n_out)]
    send_ref[...] = block_ref[pl.ds(pl.multiple_of((at ^ 1) * n_out, n_out), n_out)]


def over_sub(x, k):
    return lax.ppermute(x, "sub", [(i, i ^ k) for i in range(SUB_DEVS)])


def over_y(x):
    return [over_sub(x, 2 * d) for d in ORDER[1:]]


def over_sub_mirrored(x, k):
    pairs = []
    for z in range(4):
        for j in range(8):
            for s in range(SUB_DEVS):
                pairs.append(((8 * z + j) * SUB_DEVS + s, (8 * (3 - z) + j) * SUB_DEVS + (s ^ k)))
    return lax.ppermute(x, ("rows", "sub"), pairs)


def over_z(x):
    return [x] + [permute_rows(x, lambda i, d=d: i ^ (8 * d)) for d in ORDER[1:]]


def over_x(xs):
    return [permute_rows(x, lambda i, d=d: i ^ (2 * d)) for d, x in zip(ORDER[1:], xs)]


def per_device(embeddings, rotation, codebooks):
    n, n_feat = embeddings.shape
    width = rotation.shape[0]
    subs, _, codes = codebooks.shape
    half = subs * SUB_DIM // 2
    row_index = lax.axis_index("rows").astype(jnp.int32)
    sub = lax.axis_index("sub").astype(jnp.int32)
    core = row_index % 2
    place = jnp.stack([core, (row_index // 2) % 4, row_index, sub])

    partner = over_sub(embeddings, 1)
    own_y = over_y(embeddings)
    partner_y = over_y(partner)
    others = [partner]
    for pair in zip(own_y, partner_y):
        others += pair
    mats, mine, book, scores = call(
        load_kernel,
        (
            shape(rotation.shape, bf16),
            shape(embeddings.shape, bf16),
            shape((SUB_DIM, codes), f32),
            shape((codes, 2 * SUB_DIM), bf16),
        ),
        1,
        3,
    )(place, rotation, embeddings, codebooks)
    part = shape((4, SUB_DIM, n), bf16)
    keep, send, e_own = call(
        rotate_kernel,
        (part, part, shape((n, width), bf16)),
        1,
        SUB_DEVS + 1,
        (pltpu.VMEM((subs, SUB_DIM, n), bf16),),
    )(place, mine, *others, mats)
    recv = other_core(send)
    e_own, recv = lax.optimization_barrier((e_own, recv))
    e_oth = other_core(e_own)
    piece = shape((SUB_DIM, 2 * n), bf16)
    feats = (keep, recv, *over_x(call(join_kernel, (piece,) * 3, 0, 2)(keep, recv)))

    stats_shape = shape((SUB_DIM + 8, codes), f32)
    stats = call(first_kernel, stats_shape, 0, 6)(*feats, scores)
    book, weights, stats = call(
        second_kernel, (shape((SUB_DIM, codes), f32), shape((4, codes, 2 * n), bf16), stats_shape), 0, 10
    )(*feats, book, *over_z(stats))
    book, *rebuilt = call(rebuild_kernel, (shape((SUB_DIM, codes), f32),) + (piece,) * 4, 0, 6)(
        *over_z(stats), book, weights
    )
    chunk = shape((SUB_DIM, width), f32)
    cross = call(cross_kernel, (chunk,) * 4, 0, 6)(rebuilt[0], *over_x(rebuilt[1:]), e_own, e_oth)
    got = over_x(cross[1:])
    mine = (cross[0] + got[0]) + (got[1] + got[2])
    mine = call(sum_kernel, shape((SUB_DIM, width + codes), f32), 0, 5)(*over_z(mine), book)
    v_own, low = call(
        columns_kernel, (shape((half, width + codes), f32), shape((half, width), bf16)), 1, 4
    )(place, mine, *over_x([mine] * 3))
    book_oth = other_core(v_own[:, width:])
    partner = over_sub_mirrored(low, 1)
    c_own = pack([low] + over_y(low))
    c_oth = other_core(c_own)
    z_own = pack([partner] + over_y(partner))
    z_oth = other_core(z_own)
    piece = shape((width // ROW_DEVS, half), f32)
    keep, send, new_codebooks = call(
        polar_kernel,
        (piece, piece, shape(codebooks.shape, f32)),
        1,
        6,
        (
            pltpu.VMEM((width, 2 * width), bf16),
            pltpu.VMEM((half, width), f32),
            pltpu.VMEM((128, half), f32),
        ),
    )(place, c_own, c_oth, z_own, z_oth, v_own, book_oth)
    recv = other_core(send)
    new_rotation = jnp.where(core == 0, jnp.concatenate([keep, recv], 1), jnp.concatenate([recv, keep], 1))
    return (new_codebooks, new_rotation)


def solution(mesh):
    return jax.shard_map(
        per_device,
        mesh=mesh,
        in_specs=(P("rows", "sub"), P(None, "sub"), P("sub", None, None)),
        out_specs=(P("sub", None, None), P("rows", "sub")),
        check_vma=False,
    )
```

```python
import jax
import jax.numpy as jnp
from jax import lax
from jax.experimental import pallas as pl
from jax.experimental.pallas import tpu as pltpu
from jax.sharding import PartitionSpec as P

SUB_DIM = 16
CODES = 256
SOFTNESS = 4.0
PRIOR = 8.0
Q1, Q3, Q5 = 3.4445, -4.775, 2.0315

ROW_DEVS = 32
SUB_DEVS = 8
ORDER = (0, 2, 3, 1)
BLOCKS = (0, 1, 4, 5, 6, 7, 2, 3)

f32 = jnp.float32
bf16 = jnp.bfloat16
VMEM_LIMIT = 48 * 1024 * 1024


def call(kernel, out_shape, n_scalars, n_arrays, scratch=()):
    return pl.pallas_call(
        kernel,
        out_shape=out_shape,
        in_specs=[pl.BlockSpec(memory_space=pltpu.SMEM)] * n_scalars
        + [pl.BlockSpec(memory_space=pltpu.VMEM)] * n_arrays,
        scratch_shapes=list(scratch),
        compiler_params=pltpu.CompilerParams(vmem_limit_bytes=VMEM_LIMIT),
    )


def shape(dims, dtype):
    return jax.ShapeDtypeStruct(dims, dtype)


def dot(a, b, dims=((1,), (0,)), precision=None):
    return lax.dot_general(a, b, (dims, ((), ())), precision=precision, preferred_element_type=f32)


def permute_rows(x, to):
    return lax.ppermute(x, "rows", [(i, to(i)) for i in range(ROW_DEVS)])


def other_core(x):
    return permute_rows(x, lambda i: i ^ 1)


def load_kernel(place_ref, r_ref, e_ref, book_ref, r_out, e_out, book_out, scores_out):
    n = e_ref.shape[1]
    for k in range(SUB_DEVS):
        r_out[n * k : n * (k + 1)] = r_ref[pl.ds(pl.multiple_of((place_ref[3] ^ BLOCKS[k]) * n, n), n)]
    e_out[...] = e_ref[...]
    book = book_ref[4 * place_ref[0] + place_ref[1]]
    book_out[...] = book
    scores_out[...] = score_matrix(book)


def rotate_kernel(place_ref, *refs):
    e_refs, r_ref, keep_ref, send_ref, feats_ref, rot_ref = refs[:SUB_DEVS], *refs[SUB_DEVS:]
    n = e_refs[0].shape[1]
    for k in range(SUB_DEVS):
        feats_ref[:, n * k : n * (k + 1)] = e_refs[k][...]
    rot = dot(feats_ref[...], r_ref[...]).T.astype(bf16)
    for m in range(rot_ref.shape[0]):
        rot_ref[m] = rot[SUB_DIM * m : SUB_DIM * (m + 1)]
    core, x = place_ref[0], place_ref[1]
    for j in range(4):
        keep_ref[j] = rot_ref[4 * core + (x ^ ORDER[j])]
        send_ref[j] = rot_ref[4 * (1 - core) + (x ^ ORDER[j])]


def join_kernel(keep_ref, recv_ref, *outs):
    n = keep_ref.shape[2]
    for d, out in enumerate(outs):
        out[:, :n] = keep_ref[d + 1]
        out[:, n:] = recv_ref[d + 1]


def score_matrix(book):
    sq = 0.25 * jnp.sum(book * book, axis=0, keepdims=True)
    sq_a = sq.astype(bf16).astype(f32)
    sq_b = (sq - sq_a).astype(bf16).astype(f32)
    sq_c = (sq - sq_a) - sq_b
    low = book.astype(bf16).astype(f32)
    pad = jnp.zeros((SUB_DIM - 3, book.shape[1]), f32)
    return jnp.concatenate([0.5 * low, -sq_a, -sq_b, -sq_c, pad], axis=0).T.astype(bf16)


def assign(lhs, feats):
    rhs = jnp.concatenate([feats, jnp.ones_like(feats)], axis=0)
    logits = dot(lhs, rhs)
    e = jnp.exp(logits - jnp.max(logits, axis=0, keepdims=True))
    w = (e * (1.0 / jnp.sum(e, axis=0, keepdims=True))).astype(bf16)
    return w, dot(rhs, w, ((1,), (1,)))


def assign_all(lhs, f_refs, stats_ref, w_ref=None):
    keep_ref, recv_ref = f_refs[:2]
    n = keep_ref.shape[2]
    total = None
    for d in range(4):
        for h in range(2):
            at = slice(n * h, n * (h + 1))
            feats = f_refs[d + 1][:, at] if d else f_refs[h][0]
            w, stats = assign(lhs, feats)
            total = stats if total is None else total + stats
            if w_ref is not None:
                w_ref[d, :, at] = w
    stats_ref[...] = total[: stats_ref.shape[0]]


def first_kernel(k, r, f1, f2, f3, scores_ref, stats_ref):
    assign_all(scores_ref[...], (k, r, f1, f2, f3), stats_ref)


def new_book(a, b, c, d, book):
    stats = (a[...] + b[...]) + (c[...] + d[...])
    return (stats[:SUB_DIM] + PRIOR * book) / (stats[SUB_DIM : SUB_DIM + 1] + PRIOR)


def second_kernel(k, r, f1, f2, f3, book_ref, a, b, c, d, book_out, w_ref, stats_ref):
    book = new_book(a, b, c, d, book_ref[...])
    book_out[...] = book
    assign_all(score_matrix(book), (k, r, f1, f2, f3), stats_ref, w_ref)


def rebuild_kernel(a, b, c, d, book_ref, w_ref, book_out, *outs):
    book = new_book(a, b, c, d, book_ref[...])
    book_out[...] = book
    low = book.astype(bf16)
    for i, out in enumerate(outs):
        out[...] = dot(low, w_ref[i]).astype(bf16)


def cross_kernel(x0, x1, x2, x3, own_ref, oth_ref, *outs):
    rebuilt = jnp.concatenate([x0[...], x1[...], x2[...], x3[...]], axis=0)
    n = own_ref.shape[0]
    part = dot(rebuilt[:, :n], own_ref[...]) + dot(rebuilt[:, n:], oth_ref[...])
    for i, out in enumerate(outs):
        out[...] = part[SUB_DIM * i : SUB_DIM * (i + 1)]


def sum_kernel(a, b, c, d, book_ref, out_ref):
    n = a.shape[1]
    out_ref[:, :n] = (a[...] + b[...]) + (c[...] + d[...])
    out_ref[:, n:] = book_ref[...]


def columns_kernel(place_ref, x0, x1, x2, x3, v_ref, low_ref):
    width = low_ref.shape[1]
    n = width // SUB_DEVS
    for d, x in enumerate((x0, x1, x2, x3)):
        rows = pl.ds(pl.multiple_of((place_ref[1] ^ ORDER[d]) * SUB_DIM, SUB_DIM), SUB_DIM)
        for k in range(SUB_DEVS):
            at = pl.ds(pl.multiple_of((place_ref[3] ^ BLOCKS[k]) * n, n), n)
            block = x[:, n * k : n * (k + 1)]
            v_ref[rows, at] = block
            low_ref[rows, at] = block.astype(bf16)
        v_ref[rows, width:] = x[:, width:]


def pack_kernel(*refs):
    for i, ref in enumerate(refs[:-1]):
        refs[-1][i] = ref[...]


def pack(xs):
    return call(pack_kernel, shape((len(xs),) + xs[0].shape, xs[0].dtype), 0, len(xs))(*xs)


def polar_kernel(
    place_ref, c0, c1, c2, c3, v_ref, book_ref, keep_ref, send_ref, book_out, parts_ref, all_ref, block_ref
):
    rows, width = all_ref.shape
    core = place_ref[0]
    n = block_ref.shape[0]
    for x in range(4):
        at = slice(SUB_DIM * x, SUB_DIM * (x + 1))
        book_out[4 * core + x] = v_ref[at, width:]
        book_out[4 * (1 - core) + x] = book_ref[at]
    cols = jnp.concatenate([c[...].reshape(-1, width) for c in (c0, c1, c2, c3)], axis=0)
    gram = dot(cols.T, cols)
    eye = lax.broadcasted_iota(jnp.int32, (n, n), 0) == lax.broadcasted_iota(jnp.int32, (n, n), 1)
    diag = jnp.zeros((n, n), f32)
    for i in range(0, width, n):
        diag = diag + jnp.where(eye, gram[i : i + n, i : i + n], 0.0)
    square = jnp.sum(jnp.sum(diag, axis=0, keepdims=True), axis=1, keepdims=True) + 1e-06
    gram = gram * (1.0 / square)
    hi = gram.astype(bf16)
    parts_ref[:, :width] = hi
    parts_ref[:, width:] = (gram - hi.astype(f32)).astype(bf16)

    def times_gram(v):
        v_hi = v.astype(bf16)
        v_lo = (v - v_hi.astype(f32)).astype(bf16)
        m = v.shape[0]
        out = dot(jnp.concatenate([v_hi, v_lo], axis=0), parts_ref[...])
        return out[:m, :width] + (out[m:, :width] + out[:m, width:])

    def quintic(v):
        image = times_gram(v)
        return Q1 * v + Q3 * image + Q5 * times_gram(image)

    def times_next_gram(v):
        return quintic(times_gram(quintic(v)))

    polar = v_ref[:, :width] * (1.0 / jnp.sqrt(square))
    polar = quintic(polar)
    image = times_next_gram(polar)
    second = times_next_gram(image)
    all_ref[...] = Q1 * polar + Q3 * image + Q5 * second
    n_out = keep_ref.shape[0]
    per_block = n // n_out
    block_ref[...] = all_ref[:, pl.ds(pl.multiple_of(place_ref[2] // per_block * n, n), n)].T
    at = place_ref[2] % per_block
    keep_ref[...] = block_ref[pl.ds(pl.multiple_of(at * n_out, n_out), n_out)]
    send_ref[...] = block_ref[pl.ds(pl.multiple_of((at ^ 1) * n_out, n_out), n_out)]


def over_sub(x, k):
    return lax.ppermute(x, "sub", [(i, i ^ k) for i in range(SUB_DEVS)])


def over_y(x):
    return [over_sub(x, 2 * d) for d in ORDER[1:]]


def over_sub_mirrored(x, k):
    pairs = []
    for z in range(4):
        for j in range(8):
            for s in range(SUB_DEVS):
                pairs.append(((8 * z + j) * SUB_DEVS + s, (8 * (3 - z) + j) * SUB_DEVS + (s ^ k)))
    return lax.ppermute(x, ("rows", "sub"), pairs)


def over_z(x):
    return [x] + [permute_rows(x, lambda i, d=d: i ^ (8 * d)) for d in (3, 2, 1)]


def over_x(xs):
    return [permute_rows(x, lambda i, d=d: i ^ (2 * d)) for d, x in zip(ORDER[1:], xs)]


def per_device(embeddings, rotation, codebooks):
    n, n_feat = embeddings.shape
    width = rotation.shape[0]
    subs, _, codes = codebooks.shape
    half = subs * SUB_DIM // 2
    row_index = lax.axis_index("rows").astype(jnp.int32)
    sub = lax.axis_index("sub").astype(jnp.int32)
    core = row_index % 2
    place = jnp.stack([core, (row_index // 2) % 4, row_index, sub])

    partner = over_sub(embeddings, 1)
    own_y = over_y(embeddings)
    partner_y = over_y(partner)
    others = [partner]
    for pair in zip(own_y, partner_y):
        others += pair
    mats, mine, book, scores = call(
        load_kernel,
        (
            shape(rotation.shape, bf16),
            shape(embeddings.shape, bf16),
            shape((SUB_DIM, codes), f32),
            shape((codes, 2 * SUB_DIM), bf16),
        ),
        1,
        3,
    )(place, rotation, embeddings, codebooks)
    part = shape((4, SUB_DIM, n), bf16)
    keep, send, e_own = call(
        rotate_kernel,
        (part, part, shape((n, width), bf16)),
        1,
        SUB_DEVS + 1,
        (pltpu.VMEM((subs, SUB_DIM, n), bf16),),
    )(place, mine, *others, mats)
    recv = other_core(send)
    e_own, recv = lax.optimization_barrier((e_own, recv))
    e_oth = other_core(e_own)
    piece = shape((SUB_DIM, 2 * n), bf16)
    feats = (keep, recv, *over_x(call(join_kernel, (piece,) * 3, 0, 2)(keep, recv)))

    stats_shape = shape((SUB_DIM + 8, codes), f32)
    stats = call(first_kernel, stats_shape, 0, 6)(*feats, scores)
    book, weights, stats = call(
        second_kernel, (shape((SUB_DIM, codes), f32), shape((4, codes, 2 * n), bf16), stats_shape), 0, 10
    )(*feats, book, *over_z(stats))
    book, *rebuilt = call(rebuild_kernel, (shape((SUB_DIM, codes), f32),) + (piece,) * 4, 0, 6)(
        *over_z(stats), book, weights
    )
    chunk = shape((SUB_DIM, width), f32)
    cross = call(cross_kernel, (chunk,) * 4, 0, 6)(rebuilt[0], *over_x(rebuilt[1:]), e_own, e_oth)
    got = over_x(cross[1:])
    mine = (cross[0] + got[0]) + (got[1] + got[2])
    mine = call(sum_kernel, shape((SUB_DIM, width + codes), f32), 0, 5)(*over_z(mine), book)
    v_own, low = call(
        columns_kernel, (shape((half, width + codes), f32), shape((half, width), bf16)), 1, 4
    )(place, mine, *over_x([mine] * 3))
    book_oth = other_core(v_own[:, width:])
    partner = over_sub_mirrored(low, 1)
    c_own = pack([low] + over_y(low))
    c_oth = other_core(c_own)
    z_own = pack([partner] + over_y(partner))
    z_oth = other_core(z_own)
    piece = shape((width // ROW_DEVS, half), f32)
    keep, send, new_codebooks = call(
        polar_kernel,
        (piece, piece, shape(codebooks.shape, f32)),
        1,
        6,
        (
            pltpu.VMEM((width, 2 * width), bf16),
            pltpu.VMEM((half, width), f32),
            pltpu.VMEM((128, half), f32),
        ),
    )(place, c_own, c_oth, z_own, z_oth, v_own, book_oth)
    recv = other_core(send)
    new_rotation = jnp.where(core == 0, jnp.concatenate([keep, recv], 1), jnp.concatenate([recv, keep], 1))
    return (new_codebooks, new_rotation)


def solution(mesh):
    return jax.shard_map(
        per_device,
        mesh=mesh,
        in_specs=(P("rows", "sub"), P(None, "sub"), P("sub", None, None)),
        out_specs=(P("sub", None, None), P("rows", "sub")),
        check_vma=False,
    )
```
